32 devices in a mesh: rep: 2 (over x), tbl: 16 (over z, y, core).
Axes of the slice: x: 2, y: 2, z: 4, core: 2. Of those that a mesh axis runs over, the one named last changes fastest.
Arguments:
- embeddings: bfloat16 [131072, 256], P('tbl'), may hold values from -6 to 6
- raw_ids: int32 [128, 16, 60], P('tbl', 'rep'), may hold values from 0 to 16383
- id_weights: bfloat16 [128, 16, 60], P('tbl', 'rep'), may hold values from 0.25 to 4
- lengths: int32 [128, 16], P('tbl', 'rep'), may hold values from 1 to 60
- table_slot: int32 [16], replicated, may hold values from 0 to 15, each once
- table_rows: int32 [16], replicated, may hold values from 1 to 8192, 32768 in all
Outputs:
- pooled: float32 [128, 16, 256], P('tbl', 'rep')
The draws below stay inside these ranges and needn't reach their ends.
Inputs may be any that keep to these rules, and one draw needn't show every extreme that they name: The bag of request q for table k holds its first lengths[q, k] ids. `table_slot`: each slot holds exactly one table. `table_rows`: some table uses all 8192 rows of its slot.
All inputs are finite; a program needn't handle non-finite values.
Results may differ from the reference program's by a relative error of at most 0.0003.
Values sent between devices are 32-bit elements; how exact they have to be, the bound alone decides.
No kernel may reach another device: no remote copies, remote signals or barrier semaphores. Data moves between devices by JAX's collectives and lax.ppermute only.
A program may use at most 64 MiB of HBM per device.

```python
import math
import jax
import jax.numpy as jnp
import numpy as np
from jax import lax

D = 256
ROWS_SLOT = 8192
BAG = 60
TABLES = 16
REQUESTS = 128


def set_ends(array, rng, low, top_value):
    index_at = [jax.random.randint(jax.random.fold_in(rng, axis), (), 0, length) for axis, length in enumerate(array.shape)]
    longest = array.shape.index(max(array.shape))
    next_to = index_at[:longest] + [(index_at[longest] + 1) % array.shape[longest]] + index_at[longest + 1:]
    return array.at[tuple(index_at)].set(low).at[tuple(next_to)].set(top_value)


def shard_levels(own_key, shape, split, least, largest):
    gain = 1.0
    for position, blocks in split:
        heights = jax.random.uniform(jax.random.fold_in(jax.random.fold_in(own_key, 6), position), (blocks,), jnp.float32, least / len(split), largest / len(split))
        gain = gain * jnp.repeat(jnp.exp(heights), shape[position] // blocks).reshape((-1,) + (1,) * (len(shape) - 1 - position))
    return gain


def rank_bounds(count, skew):
    weights = [(1 << 20) // math.isqrt(standing ** skew) + 1 for standing in range(1, count + 1)]
    spread = 1 + sum(weights) // (1 << 30)
    return np.cumsum(np.array([max(1, weight // spread) for weight in weights]))


def ranked(key, dims, amount, slope):
    grid = rank_bounds(amount, slope)
    ticket = jax.random.randint(jax.random.fold_in(key, 1), dims, 0, int(grid[amount - 1]))
    standing = jnp.searchsorted(jnp.asarray(grid, jnp.int32), ticket, side="right")
    return jax.random.permutation(jax.random.fold_in(key, 2), amount)[standing].astype(jnp.int32)


def split_up(number_of, total, bound, slope):
    portions = [(1 << 20) // math.isqrt(rank ** slope) + 1 for rank in range(2, number_of + 1)]
    surplus, given = total - bound - (number_of - 1), [1] * (number_of - 1)
    while surplus > 0:
        movable = [i for i in range(number_of - 1) if given[i] < bound]
        mass, budget = sum([portions[i] for i in movable]), surplus
        for i in movable:
            more = min(bound - given[i], max(1, budget * portions[i] // mass), surplus)
            given[i] = given[i] + more
            surplus = surplus - more
    return np.array([bound] + given)


def uneven_parts(own_key, amount, total, reach, skew):
    if amount == 2:
        one = jax.random.randint(own_key, (), max(1, total - reach), min(reach, total - 1) + 1)
        return jnp.stack([one, total - one])
    sizes = jnp.asarray(split_up(amount, total, reach, skew), jnp.int32)
    pairs = (amount - 1) // 2
    donor, taker = sizes[1:1 + 2 * pairs:2], sizes[2:2 + 2 * pairs:2]
    margin = jnp.minimum(donor - 1, reach - taker)
    passed = jax.random.randint(jax.random.fold_in(own_key, 1), (pairs,), 0, 1 << 20) % (margin + 1)
    sizes = sizes.at[1:1 + 2 * pairs:2].set(donor - passed).at[2:2 + 2 * pairs:2].set(taker + passed)
    return sizes[jax.random.permutation(jax.random.fold_in(own_key, 2), amount)]


def normal_values(key, shape, deviation, limit, cuts=(), kind=jnp.bfloat16):
    entries = jax.random.normal(key, shape, jnp.float32) * deviation
    if len(cuts) > 0:
        entries = shard_levels(key, shape, cuts, -0.22, 0.18) * entries
    return jnp.clip(entries, min=-limit, max=limit).astype(kind)


def setup_inputs(seed: int = 0) -> dict:
    keys = jax.random.split(jax.random.key(seed), 7)
    embeddings = normal_values(keys[0], (TABLES * ROWS_SLOT, D), 1.0, 6.0, ((0, 16),))
    raw_ids = set_ends(ranked(keys[1], (REQUESTS, TABLES, BAG), 16384, 2), jax.random.fold_in(keys[1], 3), 0, 16383).astype(jnp.int32)
    id_weights = jnp.clip(jnp.exp(math.log(4.0) - 2.7725887 * jax.random.uniform(keys[2], (REQUESTS, TABLES, BAG), jnp.float32) ** shard_levels(keys[2], (REQUESTS, TABLES, BAG), ((0, 16), (1, 2)), -0.2, 0.2)), 0.25, 4.0).astype(jnp.bfloat16)
    lengths = set_ends(jax.random.randint(keys[3], (REQUESTS, TABLES), 1, BAG + 1), jax.random.fold_in(keys[3], 1), 1, BAG).astype(jnp.int32)
    table_slot = jax.random.permutation(keys[4], TABLES).astype(jnp.int32)
    table_rows = uneven_parts(keys[5], TABLES, TABLES * ROWS_SLOT // 4, ROWS_SLOT, 2).astype(jnp.int32)
    return dict(embeddings=embeddings, raw_ids=raw_ids, id_weights=id_weights, lengths=lengths, table_slot=table_slot, table_rows=table_rows)


def reference(embeddings, raw_ids, id_weights, lengths, table_slot, table_rows):
    positions = jnp.arange(BAG, dtype=jnp.int32)

    def pool_table(table_index):
        hashed = lax.dynamic_index_in_dim(raw_ids, table_index, 1, keepdims=False)
        weighting = lax.dynamic_index_in_dim(id_weights, table_index, 1, keepdims=False).astype(jnp.float32)
        counts = lax.dynamic_index_in_dim(lengths, table_index, 1, keepdims=False)
        targets = table_slot[table_index] * ROWS_SLOT + hashed % table_rows[table_index]
        picked = embeddings[targets].astype(jnp.float32)
        live_mask = positions[None, :] < counts[:, None]
        scaled = jnp.where(live_mask, weighting, jnp.float32(0.0))
        summed = jnp.sum(scaled[..., None] * picked, axis=1)
        return summed / counts.astype(jnp.float32)[:, None]

    pooled = lax.map(pool_table, jnp.arange(TABLES, dtype=jnp.int32))
    return jnp.transpose(pooled, (1, 0, 2))
```

```python
import functools

import jax
import jax.numpy as jnp
from jax import lax
from jax.experimental import pallas as pl
from jax.experimental.pallas import tpu as pltpu
from jax.sharding import PartitionSpec as P

LANES = 128
HALF = 64
SUB = 8
LOW = 256
BLOCK_BAGS = 64


def pack_kernel(slot_ref, rows_ref, ids_ref, weights_ref, len_ref, out_ref, wide_ref):
    queries, members, width = ids_ref.shape
    first = lax.axis_index("rep") * members
    wide_ref[:, 0:width] = weights_ref[...].reshape(queries * members, width).astype(jnp.float32)
    flat_ids = ids_ref.reshape(queries * members, width)
    position = lax.broadcasted_iota(jnp.int32, (queries, width), 1)
    counts = len_ref[...]
    out_ref[...] = jnp.zeros_like(out_ref)
    for member in range(members):
        slot = slot_ref[first + member]
        rows = jnp.full((queries, width), rows_ref[first + member], jnp.int32).astype(jnp.float32)
        ids = flat_ids[pl.ds(member, queries, stride=members), :].astype(jnp.float32)
        local = ids - jnp.floor((ids + 0.5) * (1.0 / rows)) * rows
        count = counts[:, member : member + 1]
        weights = wide_ref[pl.ds(member, queries, stride=members), 0:width]
        weights = jnp.where(position < count, weights, 0.0)
        out_ref[slot, :, 0:width] = local
        out_ref[slot, :, width : width + 1] = count.astype(jnp.float32)
        out_ref[slot, :, HALF : HALF + width] = weights


def pool_kernel(width, slot_ref, msg_ref, emb_ref, out_ref, lhs_ref, rhs_ref, w_ref):
    sources = msg_ref.shape[0]
    tables = slot_ref.shape[0]
    replicas = lax.axis_size("rep")
    here = lax.axis_index("tbl")

    def find(k, owner):
        return jnp.where(slot_ref[k] == here, k // (tables // replicas), owner)

    owner = lax.fori_loop(0, tables, find, jnp.int32(0))
    rows, dim = emb_ref.shape
    highs = rows // LOW
    per = SUB // replicas
    block = min(BLOCK_BAGS, sources * per)
    groups = block // SUB
    lane = lax.broadcasted_iota(jnp.int32, (SUB, LANES), 1)
    sub = lax.broadcasted_iota(jnp.int32, (SUB, LANES), 0)
    left = lane < HALF
    low_iota = lax.broadcasted_iota(jnp.int32, (LOW, LANES), 0).astype(jnp.float32).astype(jnp.bfloat16)

    def gather_group(start):
        one, two = msg_ref[start], msg_ref[start + 1]
        low_half = jnp.where(sub < per, one, pltpu.roll(two, per, 0))
        high_half = jnp.where(sub < per, pltpu.roll(one, per, 0), two)
        return jnp.where(owner == 0, low_half, high_half)

    def one_block(index, carry):
        base = index * (block // per)

        def one_group(g, carry):
            msg = gather_group(base + 2 * g)
            turned = pltpu.roll(msg, HALF, 1)
            ids = jnp.where(left, msg, turned)
            weights = jnp.where(left, turned, msg)
            high = jnp.floor(ids * (1.0 / LOW))
            low = ids - high * LOW
            for m in range(SUB // 2):
                cols = slice(m * LANES, (m + 1) * LANES)
                own = sub == jnp.where(left, 2 * m, 2 * m + 1)
                h = jnp.where(own, high, -100.0)
                h = jnp.concatenate([h, h - 1.0], 0).astype(jnp.bfloat16)
                w = jnp.where(own, weights, 0.0)
                w = jnp.concatenate([w, w], 0).astype(jnp.bfloat16)
                for top in range(0, highs, 2):
                    lhs_ref[top * SUB : (top + 2) * SUB, cols] = jnp.where(
                        h == jnp.bfloat16(top), w, jnp.bfloat16(0)
                    )
                row = jnp.where(left[0:1], low[2 * m : 2 * m + 1], low[2 * m + 1 : 2 * m + 2])
                row = jnp.broadcast_to(row, (16, LANES)).astype(jnp.bfloat16)
                row = jnp.concatenate([row] * (LOW // 16), 0)
                rhs_ref[:, cols] = jnp.where(low_iota == row, jnp.bfloat16(1), jnp.bfloat16(0))
            spread = lax.dot_general(
                lhs_ref[...], rhs_ref[...], (((1,), (1,)), ((), ())), preferred_element_type=jnp.float32
            )
            rest = spread - spread.astype(jnp.bfloat16).astype(jnp.float32)
            at = pl.ds(pl.multiple_of(g * 2 * SUB, 2 * SUB), 2 * SUB)
            for top in range(highs):
                part = slice(top * SUB, (top + 1) * SUB)
                both = jnp.concatenate([spread[part], rest[part]], 0)
                w_ref[at, top * LOW : (top + 1) * LOW] = both.astype(jnp.bfloat16)
            return carry

        lax.fori_loop(0, groups, one_group, 0)
        total = jnp.dot(w_ref[...], emb_ref[...], preferred_element_type=jnp.float32)
        for g in range(groups):
            msg = gather_group(base + 2 * g)
            at = 2 * SUB * g
            pooled = total[at : at + SUB] + total[at + SUB : at + 2 * SUB]
            pooled = pooled / msg[:, width : width + 1]
            first, last = pooled[:, :LANES], pooled[:, LANES:]
            one = jnp.where(sub < per, first, pltpu.roll(last, per, 0))
            two = jnp.where(sub < per, pltpu.roll(first, per, 0), last)
            for replica in range(replicas):
                out_ref[(base + 2 * g) * replicas + replica] = one
                out_ref[(base + 2 * g + 1) * replicas + replica] = two
        return carry

    blocks = sources * per // block
    if blocks == 1:
        one_block(0, 0)
    else:
        lax.fori_loop(0, blocks, one_block, 0)


def place_kernel(slot_ref, by_slot_ref, out_ref):
    queries, members, dim = out_ref.shape
    first = lax.axis_index("rep") * members
    per = by_slot_ref.shape[1] // 2
    upper = lax.broadcasted_iota(jnp.int32, by_slot_ref.shape[1:], 0) < per
    for member in range(members):
        slot = slot_ref[first + member]
        one, two = by_slot_ref[2 * slot], by_slot_ref[2 * slot + 1]
        out_ref[:, member, :LANES] = jnp.where(upper, one, pltpu.roll(two, per, 0))
        out_ref[:, member, LANES:] = jnp.where(upper, pltpu.roll(one, per, 0), two)


def exchange(array):
    return lax.all_to_all(array, ("tbl", "rep"), split_axis=0, concat_axis=0, tiled=True)


def per_device(embeddings, raw_ids, id_weights, lengths, table_slot, table_rows):
    queries, members, width = raw_ids.shape
    tables = table_slot.shape[0]
    rows, dim = embeddings.shape
    vmem = pl.BlockSpec(memory_space=pltpu.VMEM)
    smem = pl.BlockSpec(memory_space=pltpu.SMEM)
    message = pl.pallas_call(
        pack_kernel,
        out_shape=jax.ShapeDtypeStruct((tables, queries, LANES), jnp.float32),
        in_specs=[smem, smem, vmem, vmem, vmem],
        out_specs=vmem,
        scratch_shapes=[pltpu.VMEM((queries * members, LANES), jnp.float32)],
        name="pack",
    )(table_slot, table_rows, raw_ids, id_weights, lengths)
    replicas = lax.axis_size("rep")
    split = message.reshape(tables * replicas, queries // replicas, LANES)
    received = exchange(split).reshape(message.shape)
    block = min(BLOCK_BAGS, tables * SUB // 2)
    pooled = pl.pallas_call(
        functools.partial(pool_kernel, width),
        out_shape=jax.ShapeDtypeStruct((tables * replicas, SUB, LANES), jnp.float32),
        in_specs=[smem, vmem, vmem],
        out_specs=vmem,
        scratch_shapes=[
            pltpu.VMEM((rows // LOW * SUB, SUB * HALF), jnp.bfloat16),
            pltpu.VMEM((LOW, SUB * HALF), jnp.bfloat16),
            pltpu.VMEM((2 * block, rows), jnp.bfloat16),
        ],
        name="pool",
    )(table_slot, received, embeddings)
    by_slot = exchange(pooled)
    return pl.pallas_call(
        place_kernel,
        out_shape=jax.ShapeDtypeStruct((queries, members, dim), jnp.float32),
        in_specs=[smem, vmem],
        out_specs=vmem,
        name="place",
    )(table_slot, by_slot)


def solution(mesh):
    in_specs = (
        P("tbl", None),
        P("tbl", "rep", None),
        P("tbl", "rep", None),
        P("tbl", "rep"),
        P(),
        P(),
    )
    out_specs = P("tbl", "rep", None)
    return jax.shard_map(
        per_device, mesh=mesh, in_specs=in_specs, out_specs=out_specs, check_vma=False
    )
```

```python
import functools

import jax
import jax.numpy as jnp
from jax import lax
from jax.experimental import pallas as pl
from jax.experimental.pallas import tpu as pltpu
from jax.sharding import PartitionSpec as P

LANES = 128
HALF = 64
SUB = 8
LOW = 256
BLOCK_BAGS = 64


def fetch(pairs, sems):
    copies = [pltpu.make_async_copy(src, dst, sems.at[i]) for i, (src, dst) in enumerate(pairs)]
    for copy in copies:
        copy.start()
    for copy in copies:
        copy.wait()


def pack_kernel(
    slot_hbm, rows_hbm, ids_hbm, weights_hbm, len_hbm, out_ref,
    slot_ref, rows_ref, ids_ref, weights_ref, len_ref, wide_ref, sems,
):
    pairs = (
        (slot_hbm, slot_ref), (rows_hbm, rows_ref), (ids_hbm, ids_ref),
        (weights_hbm, weights_ref), (len_hbm, len_ref),
    )
    fetch(pairs, sems)
    queries, members, width = ids_ref.shape
    first = lax.axis_index("rep") * members
    wide_ref[:, 0:width] = weights_ref[...].reshape(queries * members, width).astype(jnp.float32)
    flat_ids = ids_ref.reshape(queries * members, width)
    position = lax.broadcasted_iota(jnp.int32, (queries, width), 1)
    counts = len_ref[...]
    out_ref[...] = jnp.zeros_like(out_ref)
    for member in range(members):
        slot = slot_ref[first + member]
        rows = jnp.full((queries, width), rows_ref[first + member], jnp.int32).astype(jnp.float32)
        ids = flat_ids[pl.ds(member, queries, stride=members), :].astype(jnp.float32)
        local = ids - jnp.floor((ids + 0.5) * (1.0 / rows)) * rows
        count = counts[:, member : member + 1]
        weights = wide_ref[pl.ds(member, queries, stride=members), 0:width]
        weights = jnp.where(position < count, weights, 0.0)
        out_ref[slot, :, 0:width] = local
        out_ref[slot, :, width : width + 1] = count.astype(jnp.float32)
        out_ref[slot, :, HALF : HALF + width] = weights


def pool_kernel(width, slot_hbm, msg_ref, emb_hbm, out_ref, slot_ref, emb_ref, lhs_ref, rhs_ref, w_ref, sems):
    slot_copy = pltpu.make_async_copy(slot_hbm, slot_ref, sems.at[0])
    emb_copy = pltpu.make_async_copy(emb_hbm, emb_ref, sems.at[1])
    slot_copy.start()
    emb_copy.start()
    sources = msg_ref.shape[0]
    tables = slot_ref.shape[0]
    replicas = lax.axis_size("rep")
    here = lax.axis_index("tbl")

    def find(k, owner):
        return jnp.where(slot_ref[k] == here, k // (tables // replicas), owner)

    slot_copy.wait()
    owner = lax.fori_loop(0, tables, find, jnp.int32(0))
    rows, dim = emb_ref.shape
    highs = rows // LOW
    per = SUB // replicas
    block = min(BLOCK_BAGS, sources * per)
    groups = block // SUB
    lane = lax.broadcasted_iota(jnp.int32, (SUB, LANES), 1)
    sub = lax.broadcasted_iota(jnp.int32, (SUB, LANES), 0)
    left = lane < HALF
    low_iota = lax.broadcasted_iota(jnp.int32, (LOW, LANES), 0).astype(jnp.float32).astype(jnp.bfloat16)

    def gather_group(start):
        one, two = msg_ref[start], msg_ref[start + 1]
        low_half = jnp.where(sub < per, one, pltpu.roll(two, per, 0))
        high_half = jnp.where(sub < per, pltpu.roll(one, per, 0), two)
        return jnp.where(owner == 0, low_half, high_half)

    def one_block(index, carry):
        base = index * (block // per)

        def one_group(g, carry):
            msg = gather_group(base + 2 * g)
            turned = pltpu.roll(msg, HALF, 1)
            ids = jnp.where(left, msg, turned)
            weights = jnp.where(left, turned, msg)
            high = jnp.floor(ids * (1.0 / LOW))
            low = ids - high * LOW
            for m in range(SUB // 2):
                cols = slice(m * LANES, (m + 1) * LANES)
                own = sub == jnp.where(left, 2 * m, 2 * m + 1)
                h = jnp.where(own, high, -100.0)
                h = jnp.concatenate([h, h - 1.0], 0).astype(jnp.bfloat16)
                w = jnp.where(own, weights, 0.0)
                w = jnp.concatenate([w, w], 0).astype(jnp.bfloat16)
                for top in range(0, highs, 2):
                    lhs_ref[top * SUB : (top + 2) * SUB, cols] = jnp.where(
                        h == jnp.bfloat16(top), w, jnp.bfloat16(0)
                    )
                row = jnp.where(left[0:1], low[2 * m : 2 * m + 1], low[2 * m + 1 : 2 * m + 2])
                row = jnp.broadcast_to(row, (16, LANES)).astype(jnp.bfloat16)
                row = jnp.concatenate([row] * (LOW // 16), 0)
                rhs_ref[:, cols] = jnp.where(low_iota == row, jnp.bfloat16(1), jnp.bfloat16(0))
            spread = lax.dot_general(
                lhs_ref[...], rhs_ref[...], (((1,), (1,)), ((), ())), preferred_element_type=jnp.float32
            )
            rest = spread - spread.astype(jnp.bfloat16).astype(jnp.float32)
            at = pl.ds(pl.multiple_of(g * 2 * SUB, 2 * SUB), 2 * SUB)
            for top in range(highs):
                part = slice(top * SUB, (top + 1) * SUB)
                both = jnp.concatenate([spread[part], rest[part]], 0)
                w_ref[at, top * LOW : (top + 1) * LOW] = both.astype(jnp.bfloat16)
            return carry

        lax.fori_loop(0, groups, one_group, 0)
        pl.when(index == 0)(emb_copy.wait)
        total = jnp.dot(w_ref[...], emb_ref[...], preferred_element_type=jnp.float32)
        for g in range(groups):
            msg = gather_group(base + 2 * g)
            at = 2 * SUB * g
            pooled = total[at : at + SUB] + total[at + SUB : at + 2 * SUB]
            pooled = pooled / msg[:, width : width + 1]
            first, last = pooled[:, :LANES], pooled[:, LANES:]
            one = jnp.where(sub < per, first, pltpu.roll(last, per, 0))
            two = jnp.where(sub < per, pltpu.roll(first, per, 0), last)
            for replica in range(replicas):
                out_ref[(base + 2 * g) * replicas + replica] = one
                out_ref[(base + 2 * g + 1) * replicas + replica] = two
        return carry

    blocks = sources * per // block
    if blocks == 1:
        one_block(0, 0)
    else:
        lax.fori_loop(0, blocks, one_block, 0)


def place_kernel(slot_hbm, by_slot_ref, out_ref, slot_ref, sems):
    fetch(((slot_hbm, slot_ref),), sems)
    queries, members, dim = out_ref.shape
    first = lax.axis_index("rep") * members
    per = by_slot_ref.shape[1] // 2
    upper = lax.broadcasted_iota(jnp.int32, by_slot_ref.shape[1:], 0) < per
    for member in range(members):
        slot = slot_ref[first + member]
        one, two = by_slot_ref[2 * slot], by_slot_ref[2 * slot + 1]
        out_ref[:, member, :LANES] = jnp.where(upper, one, pltpu.roll(two, per, 0))
        out_ref[:, member, LANES:] = jnp.where(upper, pltpu.roll(one, per, 0), two)


def exchange(array):
    return lax.all_to_all(array, ("tbl", "rep"), split_axis=0, concat_axis=0, tiled=True)


def per_device(embeddings, raw_ids, id_weights, lengths, table_slot, table_rows):
    pinned = (embeddings, raw_ids, id_weights, lengths, table_slot, table_rows)
    embeddings, raw_ids, id_weights, lengths, table_slot, table_rows = (
        pltpu.with_memory_space_constraint(x, pltpu.HBM) for x in pinned
    )
    queries, members, width = raw_ids.shape
    tables = table_slot.shape[0]
    rows, dim = embeddings.shape
    vmem = pl.BlockSpec(memory_space=pltpu.VMEM)
    hbm = pl.BlockSpec(memory_space=pltpu.HBM)
    slots = pltpu.SMEM(table_slot.shape, jnp.int32)
    message = pl.pallas_call(
        pack_kernel,
        out_shape=jax.ShapeDtypeStruct((tables, queries, LANES), jnp.float32),
        in_specs=[hbm] * 5,
        out_specs=vmem,
        scratch_shapes=[
            slots,
            slots,
            pltpu.VMEM(raw_ids.shape, raw_ids.dtype),
            pltpu.VMEM(id_weights.shape, id_weights.dtype),
            pltpu.VMEM(lengths.shape, lengths.dtype),
            pltpu.VMEM((queries * members, LANES), jnp.float32),
            pltpu.SemaphoreType.DMA((5,)),
        ],
        compiler_params=pltpu.CompilerParams(vmem_limit_bytes=2 << 20),
        name="pack",
    )(table_slot, table_rows, raw_ids, id_weights, lengths)
    replicas = lax.axis_size("rep")
    split = message.reshape(tables * replicas, queries // replicas, LANES)
    received = exchange(split).reshape(message.shape)
    block = min(BLOCK_BAGS, tables * SUB // 2)
    pooled = pl.pallas_call(
        functools.partial(pool_kernel, width),
        out_shape=jax.ShapeDtypeStruct((tables * replicas, SUB, LANES), jnp.float32),
        in_specs=[hbm, vmem, hbm],
        out_specs=vmem,
        scratch_shapes=[
            slots,
            pltpu.VMEM(embeddings.shape, embeddings.dtype),
            pltpu.VMEM((rows // LOW * SUB, SUB * HALF), jnp.bfloat16),
            pltpu.VMEM((LOW, SUB * HALF), jnp.bfloat16),
            pltpu.VMEM((2 * block, rows), jnp.bfloat16),
            pltpu.SemaphoreType.DMA((2,)),
        ],
        compiler_params=pltpu.CompilerParams(vmem_limit_bytes=24 << 20),
        name="pool",
    )(table_slot, received, embeddings)
    by_slot = exchange(pooled)
    return pl.pallas_call(
        place_kernel,
        out_shape=jax.ShapeDtypeStruct((queries, members, dim), jnp.float32),
        in_specs=[hbm, vmem],
        out_specs=vmem,
        scratch_shapes=[slots, pltpu.SemaphoreType.DMA((1,))],
        compiler_params=pltpu.CompilerParams(vmem_limit_bytes=2 << 20),
        name="place",
    )(table_slot, by_slot)


def solution(mesh):
    in_specs = (
        P("tbl", None),
        P("tbl", "rep", None),
        P("tbl", "rep", None),
        P("tbl", "rep"),
        P(),
        P(),
    )
    out_specs = P("tbl", "rep", None)
    return jax.shard_map(
        per_device, mesh=mesh, in_specs=in_specs, out_specs=out_specs, check_vma=False
    )
```

```python
import functools

import jax
import jax.numpy as jnp
import numpy as np
from jax import lax
from jax.experimental import pallas as pl
from jax.experimental.pallas import tpu as pltpu
from jax.sharding import PartitionSpec as P

LANES = 128
HALF = 64
SUB = 8
LOW = 256
BLOCK_BAGS = 64
UNROLL = 4
CHUNKS = 8
ORDER_SEED = 217


def block_order(shards):
    return np.random.RandomState(ORDER_SEED).permutation(shards)


def fetch(pairs, sems):
    copies = [pltpu.make_async_copy(src, dst, sems.at[i]) for i, (src, dst) in enumerate(pairs)]
    for copy in copies:
        copy.start()
    for copy in copies:
        copy.wait()


def pack_kernel(
    place_hbm, slot_hbm, rows_hbm, ids_hbm, weights_hbm, len_hbm, out_ref, info_ref,
    place_ref, slot_ref, rows_ref, ids_ref, weights_ref, len_ref, wide_ref, sems,
):
    pairs = (
        (place_hbm, place_ref), (slot_hbm, slot_ref), (rows_hbm, rows_ref), (ids_hbm, ids_ref),
        (weights_hbm, weights_ref), (len_hbm, len_ref),
    )
    fetch(pairs, sems)
    queries, members, width = ids_ref.shape
    first = lax.axis_index("rep") * members
    wide_ref[:, 0:width] = weights_ref[...].reshape(queries * members, width).astype(jnp.float32)
    flat_ids = ids_ref.reshape(queries * members, width)
    position = lax.broadcasted_iota(jnp.int32, (queries, width), 1)
    counts = len_ref[...]
    out_ref[...] = jnp.zeros_like(out_ref)
    here = lax.axis_index("tbl")
    lane = lax.broadcasted_iota(jnp.int32, (1, LANES), 1)

    def find(k, owner):
        return jnp.where(slot_ref[k] == here, k // members, owner)

    owner = lax.fori_loop(0, slot_ref.shape[0], find, jnp.int32(0), unroll=slot_ref.shape[0] <= 16)
    info_ref[1:2, :] = jnp.full((1, LANES), owner, jnp.int32)
    mine = jnp.zeros((1, LANES), jnp.int32)
    for member in range(members):
        place = place_ref[slot_ref[first + member]]
        mine = jnp.where(lane == member, place, mine)
        rows = jnp.full((queries, width), rows_ref[first + member], jnp.int32).astype(jnp.float32)
        ids = flat_ids[pl.ds(member, queries, stride=members), :].astype(jnp.float32)
        local = ids - jnp.floor((ids + 0.5) * (1.0 / rows)) * rows
        count = counts[:, member : member + 1]
        weights = wide_ref[pl.ds(member, queries, stride=members), 0:width]
        weights = jnp.where(position < count, weights, 0.0)
        out_ref[place, :, 0:width] = local
        out_ref[place, :, width : width + 1] = count.astype(jnp.float32)
        out_ref[place, :, HALF : HALF + width] = weights
    info_ref[0:1, :] = mine


def pool_kernel(width, info_ref, msg_ref, emb_hbm, out_ref, emb_ref, w_ref, sems):
    rows, dim = emb_ref.shape
    highs = rows // LOW
    chunks = sems.shape[0]
    size = rows // chunks
    copies = [
        pltpu.make_async_copy(emb_hbm.at[pl.ds(c * size, size)], emb_ref.at[pl.ds(c * size, size)], sems.at[c])
        for c in range(chunks)
    ]
    for copy in copies:
        copy.start()
    sources = msg_ref.shape[0]
    replicas = lax.axis_size("rep")
    per = SUB // replicas
    block = min(BLOCK_BAGS, sources * per)
    groups = block // SUB
    lane = lax.broadcasted_iota(jnp.int32, (SUB, LANES), 1)
    sub = lax.broadcasted_iota(jnp.int32, (SUB, LANES), 0)
    left = lane < HALF
    upper = sub < per
    first_owner = jnp.broadcast_to(info_ref[1:2, :], (SUB, LANES)) == 0
    owns = [sub % per == jnp.where(left, 2 * m, 2 * m + 1) for m in range(2)]
    low_iota = lax.broadcasted_iota(jnp.int32, (LOW, LANES), 0).astype(jnp.float32).astype(jnp.bfloat16)

    def gather_group(start):
        one, two = msg_ref[start], msg_ref[start + 1]
        low_half = jnp.where(upper, one, pltpu.roll(two, per, 0))
        high_half = jnp.where(upper, pltpu.roll(one, per, 0), two)
        return jnp.where(first_owner, low_half, high_half)

    def spread_four(high, low, weights, flip, base):
        lhs, rhs = [], []
        shift = jnp.where(upper, 1.0, 0.0) if flip else jnp.where(upper, 0.0, 1.0)
        for m in range(2):
            h = jnp.where(owns[m], high - shift, -100.0)
            h = jnp.concatenate([h, h - 2.0], 0).astype(jnp.bfloat16)
            w = jnp.where(owns[m], weights, 0.0)
            w = jnp.concatenate([w, w], 0).astype(jnp.bfloat16)
            lhs.append(
                jnp.concatenate(
                    [jnp.where(h == jnp.bfloat16(top), w, jnp.bfloat16(0)) for top in range(0, highs, 4)], 0
                )
            )
            at = base + 2 * m
            row = jnp.where(left[0:1], low[at : at + 1], low[at + 1 : at + 2])
            row = jnp.broadcast_to(row, (2 * SUB, LANES)).astype(jnp.bfloat16)
            row = jnp.concatenate([row] * (LOW // (2 * SUB)), 0)
            rhs.append(jnp.where(low_iota == row, jnp.bfloat16(1), jnp.bfloat16(0)))
        return lax.dot_general(
            jnp.concatenate(lhs, 1), jnp.concatenate(rhs, 1), (((1,), (1,)), ((), ())),
            preferred_element_type=jnp.float32,
        )

    def one_block(index):
        base = index * (block // per)

        def one_group(g):
            msg = gather_group(base + 2 * g)
            turned = pltpu.roll(msg, HALF, 1)
            ids = jnp.where(left, msg, turned)
            weights = jnp.where(left, turned, msg)
            high = jnp.floor(ids * (1.0 / LOW))
            low = ids - high * LOW
            high_turned = pltpu.roll(high, per, 0)
            weights_turned = pltpu.roll(weights, per, 0)
            one = spread_four(
                jnp.where(upper, high, high_turned), low, jnp.where(upper, weights, weights_turned), False, 0
            )
            two = spread_four(
                jnp.where(upper, high_turned, high), low, jnp.where(upper, weights_turned, weights), True, per
            )
            at = pl.ds(pl.multiple_of(g * 2 * SUB, 2 * SUB), 2 * SUB)
            for v in range(highs // 2):
                for part in range(LOW // LANES):
                    cut = (slice(v * SUB, (v + 1) * SUB), slice(part * LANES, (part + 1) * LANES))
                    even = jnp.where(upper, one[cut], two[cut])
                    odd = jnp.where(upper, two[cut], one[cut])
                    both = jnp.concatenate([even, odd], 0)
                    rest = both - both.astype(jnp.bfloat16).astype(jnp.float32)
                    w_ref[0, v, part, at, :] = jnp.concatenate([even, rest[:SUB]], 0).astype(jnp.bfloat16)
                    w_ref[1, v, part, at, :] = jnp.concatenate([odd, rest[SUB:]], 0).astype(jnp.bfloat16)

        def body(g, carry):
            for u in range(UNROLL):
                one_group(g * UNROLL + u)
            return carry

        if groups == UNROLL:
            body(0, 0)
        else:
            lax.fori_loop(0, groups // UNROLL, body, 0)
        totals = [None, None]
        for c in range(chunks):
            pl.when(index == 0)(copies[c].wait)
            for parity in range(2):
                left_side, right_side = [], []
                for v in range(c * size // LOW // 2, (c + 1) * size // LOW // 2):
                    for part in range(LOW // LANES):
                        left_side.append(w_ref[parity, v, part])
                    at = (2 * v + parity) * LOW
                    right_side.append(emb_ref[at : at + LOW, :])
                term = jnp.dot(
                    jnp.concatenate(left_side, 1), jnp.concatenate(right_side, 0),
                    preferred_element_type=jnp.float32,
                )
                totals[parity] = term if c == 0 else totals[parity] + term
        for g in range(groups):
            msg = gather_group(base + 2 * g)
            at = 2 * SUB * g
            even, odd = (t[at : at + SUB] + t[at + SUB : at + 2 * SUB] for t in totals)
            pooled = (even + pltpu.roll(odd, per, 0)) / msg[:, width : width + 1]
            first, last = pooled[:, :LANES], pooled[:, LANES:]
            one = jnp.where(upper, first, pltpu.roll(last, per, 0))
            two = jnp.where(upper, pltpu.roll(first, per, 0), last)
            for replica in range(replicas):
                out_ref[(base + 2 * g) * replicas + replica] = one
                out_ref[(base + 2 * g + 1) * replicas + replica] = two

    blocks = sources * per // block
    if blocks == 1:
        one_block(0)
    else:
        pl.loop(0, blocks)(one_block)


def place_kernel(info_ref, by_slot_ref, out_ref):
    queries, members, dim = out_ref.shape
    per = by_slot_ref.shape[1] // 2
    upper = lax.broadcasted_iota(jnp.int32, by_slot_ref.shape[1:], 0) < per
    info = info_ref[0:1, :]
    for member in range(members):
        place = info[0, member]
        one, two = by_slot_ref[2 * place], by_slot_ref[2 * place + 1]
        out_ref[:, member, :LANES] = jnp.where(upper, one, pltpu.roll(two, per, 0))
        out_ref[:, member, LANES:] = jnp.where(upper, pltpu.roll(one, per, 0), two)


def exchange(array):
    shards, replicas = lax.axis_size("tbl"), lax.axis_size("rep")
    group = [int(shard) + shards * replica for shard in block_order(shards) for replica in range(replicas)]
    return lax.all_to_all(
        array, ("rep", "tbl"), split_axis=0, concat_axis=0, axis_index_groups=[group], tiled=True
    )


def per_device(embeddings, raw_ids, id_weights, lengths, table_slot, table_rows):
    places = jnp.asarray(np.argsort(block_order(lax.axis_size("tbl"))), jnp.int32)
    pinned = (embeddings, raw_ids, id_weights, lengths, table_slot, table_rows, places)
    embeddings, raw_ids, id_weights, lengths, table_slot, table_rows, places = (
        pltpu.with_memory_space_constraint(x, pltpu.HBM) for x in pinned
    )
    queries, members, width = raw_ids.shape
    tables = table_slot.shape[0]
    rows, dim = embeddings.shape
    vmem = pl.BlockSpec(memory_space=pltpu.VMEM)
    hbm = pl.BlockSpec(memory_space=pltpu.HBM)
    slots = pltpu.SMEM(table_slot.shape, jnp.int32)
    message, info = pl.pallas_call(
        pack_kernel,
        out_shape=(
            jax.ShapeDtypeStruct((tables, queries, LANES), jnp.float32),
            jax.ShapeDtypeStruct((SUB, LANES), jnp.int32),
        ),
        in_specs=[hbm] * 6,
        out_specs=(vmem, vmem),
        scratch_shapes=[
            slots,
            slots,
            slots,
            pltpu.VMEM(raw_ids.shape, raw_ids.dtype),
            pltpu.VMEM(id_weights.shape, id_weights.dtype),
            pltpu.VMEM(lengths.shape, lengths.dtype),
            pltpu.VMEM((queries * members, LANES), jnp.float32),
            pltpu.SemaphoreType.DMA((6,)),
        ],
        compiler_params=pltpu.CompilerParams(vmem_limit_bytes=4 << 20),
        name="pack",
    )(places, table_slot, table_rows, raw_ids, id_weights, lengths)
    replicas = lax.axis_size("rep")
    split = message.reshape(tables * replicas, queries // replicas, LANES)
    received = exchange(split).reshape(message.shape)
    block = min(BLOCK_BAGS, tables * SUB // 2)
    pooled = pl.pallas_call(
        functools.partial(pool_kernel, width),
        out_shape=jax.ShapeDtypeStruct((tables * replicas, SUB, LANES), jnp.float32),
        in_specs=[vmem, vmem, hbm],
        out_specs=vmem,
        scratch_shapes=[
            pltpu.VMEM(embeddings.shape, embeddings.dtype),
            pltpu.VMEM((2, rows // LOW // 2, LOW // LANES, 2 * block, LANES), jnp.bfloat16),
            pltpu.SemaphoreType.DMA((CHUNKS,)),
        ],
        compiler_params=pltpu.CompilerParams(vmem_limit_bytes=24 << 20),
        name="pool",
    )(info, received, embeddings)
    by_slot = exchange(pooled)
    return pl.pallas_call(
        place_kernel,
        out_shape=jax.ShapeDtypeStruct((queries, members, dim), jnp.float32),
        in_specs=[vmem, vmem],
        out_specs=vmem,
        compiler_params=pltpu.CompilerParams(vmem_limit_bytes=4 << 20),
        name="place",
    )(info, by_slot)


def solution(mesh):
    in_specs = (
        P("tbl", None),
        P("tbl", "rep", None),
        P("tbl", "rep", None),
        P("tbl", "rep"),
        P(),
        P(),
    )
    out_specs = P("tbl", "rep", None)
    return jax.shard_map(
        per_device, mesh=mesh, in_specs=in_specs, out_specs=out_specs, check_vma=False
    )
```

```python
import functools

import jax
import jax.numpy as jnp
import numpy as np
from jax import lax
from jax.experimental import pallas as pl
from jax.experimental.pallas import tpu as pltpu
from jax.sharding import PartitionSpec as P

LANES = 128
HALF = 64
SUB = 8
LOW = 256
BLOCK_BAGS = 64
UNROLL = 4
CHUNKS = 8
PREFIXES = (4, 6, 8)
ORDER_SEED = 217


def block_order(shards):
    return np.random.RandomState(ORDER_SEED).permutation(shards)


def fetch(pairs, sems):
    copies = [pltpu.make_async_copy(src, dst, sems.at[i]) for i, (src, dst) in enumerate(pairs)]
    for copy in copies:
        copy.start()
    for copy in copies:
        copy.wait()


def pack_kernel(
    place_hbm, slot_hbm, rows_hbm, ids_hbm, weights_hbm, len_hbm, out_ref, info_ref,
    place_ref, slot_ref, rows_ref, ids_ref, weights_ref, len_ref, wide_ref, sems,
):
    pairs = (
        (place_hbm, place_ref), (slot_hbm, slot_ref), (rows_hbm, rows_ref), (ids_hbm, ids_ref),
        (weights_hbm, weights_ref), (len_hbm, len_ref),
    )
    fetch(pairs, sems)
    queries, members, width = ids_ref.shape
    first = lax.axis_index("rep") * members
    wide_ref[:, 0:width] = weights_ref[...].reshape(queries * members, width).astype(jnp.float32)
    flat_ids = ids_ref.reshape(queries * members, width)
    position = lax.broadcasted_iota(jnp.int32, (queries, width), 1)
    counts = len_ref[...]
    out_ref[...] = jnp.zeros_like(out_ref)
    here = lax.axis_index("tbl")
    lane = lax.broadcasted_iota(jnp.int32, (1, LANES), 1)

    def find(k, table):
        return jnp.where(slot_ref[k] == here, k, table)

    table = lax.fori_loop(0, slot_ref.shape[0], find, jnp.int32(0), unroll=slot_ref.shape[0] <= 16)
    info_ref[1:2, :] = jnp.full((1, LANES), table // members, jnp.int32)
    info_ref[2:3, :] = jnp.full((1, LANES), rows_ref[table], jnp.int32)
    mine = jnp.zeros((1, LANES), jnp.int32)
    for member in range(members):
        place = place_ref[slot_ref[first + member]]
        mine = jnp.where(lane == member, place, mine)
        rows = jnp.full((queries, width), rows_ref[first + member], jnp.int32).astype(jnp.float32)
        ids = flat_ids[pl.ds(member, queries, stride=members), :].astype(jnp.float32)
        local = ids - jnp.floor((ids + 0.5) * (1.0 / rows)) * rows
        count = counts[:, member : member + 1]
        weights = wide_ref[pl.ds(member, queries, stride=members), 0:width]
        weights = jnp.where(position < count, weights, 0.0)
        out_ref[place, :, 0:width] = local
        out_ref[place, :, width : width + 1] = count.astype(jnp.float32)
        out_ref[place, :, HALF : HALF + width] = weights
    info_ref[0:1, :] = mine


def pool_kernel(width, info_ref, msg_ref, emb_hbm, out_ref, emb_ref, w_ref, sems):
    rows, dim = emb_ref.shape
    highs = rows // LOW
    chunks = sems.shape[0]
    size = rows // chunks
    copies = [
        pltpu.make_async_copy(emb_hbm.at[pl.ds(c * size, size)], emb_ref.at[pl.ds(c * size, size)], sems.at[c])
        for c in range(chunks)
    ]
    for copy in copies[: PREFIXES[0]]:
        copy.start()
    used = info_ref[2:3, :][0, 0]

    def within(part):
        low_end = 0 if part == 0 else PREFIXES[part - 1] * size
        above = used > low_end
        return above if part == len(PREFIXES) - 1 else above & (used <= PREFIXES[part] * size)

    for part in range(1, len(PREFIXES)):

        @pl.when(used > PREFIXES[part - 1] * size)
        def _(part=part):
            for copy in copies[PREFIXES[part - 1] : PREFIXES[part]]:
                copy.start()

    sources = msg_ref.shape[0]
    replicas = lax.axis_size("rep")
    per = SUB // replicas
    block = min(BLOCK_BAGS, sources * per)
    groups = block // SUB
    lane = lax.broadcasted_iota(jnp.int32, (SUB, LANES), 1)
    sub = lax.broadcasted_iota(jnp.int32, (SUB, LANES), 0)
    left = lane < HALF
    upper = sub < per
    first_owner = jnp.broadcast_to(info_ref[1:2, :], (SUB, LANES)) == 0
    owns = [sub % per == jnp.where(left, 2 * m, 2 * m + 1) for m in range(2)]
    low_iota = lax.broadcasted_iota(jnp.int32, (LOW, LANES), 0).astype(jnp.float32).astype(jnp.bfloat16)

    def gather_group(start):
        one, two = msg_ref[start], msg_ref[start + 1]
        low_half = jnp.where(upper, one, pltpu.roll(two, per, 0))
        high_half = jnp.where(upper, pltpu.roll(one, per, 0), two)
        return jnp.where(first_owner, low_half, high_half)

    def spread_four(high, low, weights, flip, base):
        lhs, rhs = [], []
        shift = jnp.where(upper, 1.0, 0.0) if flip else jnp.where(upper, 0.0, 1.0)
        for m in range(2):
            h = jnp.where(owns[m], high - shift, -100.0)
            h = jnp.concatenate([h, h - 2.0], 0).astype(jnp.bfloat16)
            w = jnp.where(owns[m], weights, 0.0)
            w = jnp.concatenate([w, w], 0).astype(jnp.bfloat16)
            lhs.append(
                jnp.concatenate(
                    [jnp.where(h == jnp.bfloat16(top), w, jnp.bfloat16(0)) for top in range(0, highs, 4)], 0
                )
            )
            at = base + 2 * m
            row = jnp.where(left[0:1], low[at : at + 1], low[at + 1 : at + 2])
            row = jnp.broadcast_to(row, (2 * SUB, LANES)).astype(jnp.bfloat16)
            row = jnp.concatenate([row] * (LOW // (2 * SUB)), 0)
            rhs.append(jnp.where(low_iota == row, jnp.bfloat16(1), jnp.bfloat16(0)))
        return lax.dot_general(
            jnp.concatenate(lhs, 1), jnp.concatenate(rhs, 1), (((1,), (1,)), ((), ())),
            preferred_element_type=jnp.float32,
        )

    def one_block(index):
        base = index * (block // per)

        def one_group(g):
            msg = gather_group(base + 2 * g)
            turned = pltpu.roll(msg, HALF, 1)
            ids = jnp.where(left, msg, turned)
            weights = jnp.where(left, turned, msg)
            high = jnp.floor(ids * (1.0 / LOW))
            low = ids - high * LOW
            high_turned = pltpu.roll(high, per, 0)
            weights_turned = pltpu.roll(weights, per, 0)
            one = spread_four(
                jnp.where(upper, high, high_turned), low, jnp.where(upper, weights, weights_turned), False, 0
            )
            two = spread_four(
                jnp.where(upper, high_turned, high), low, jnp.where(upper, weights_turned, weights), True, per
            )
            at = pl.ds(pl.multiple_of(g * 2 * SUB, 2 * SUB), 2 * SUB)
            for v in range(highs // 2):
                for part in range(LOW // LANES):
                    cut = (slice(v * SUB, (v + 1) * SUB), slice(part * LANES, (part + 1) * LANES))
                    even = jnp.where(upper, one[cut], two[cut])
                    odd = jnp.where(upper, two[cut], one[cut])
                    both = jnp.concatenate([even, odd], 0)
                    rest = both - both.astype(jnp.bfloat16).astype(jnp.float32)
                    w_ref[0, v, part, at, :] = jnp.concatenate([even, rest[:SUB]], 0).astype(jnp.bfloat16)
                    w_ref[1, v, part, at, :] = jnp.concatenate([odd, rest[SUB:]], 0).astype(jnp.bfloat16)

        def body(g, carry):
            for u in range(UNROLL):
                one_group(g * UNROLL + u)
            return carry

        if groups == UNROLL:
            body(0, 0)
        else:
            lax.fori_loop(0, groups // UNROLL, body, 0)
        for part, count in enumerate(PREFIXES):
            pl.when(within(part))(functools.partial(finish, index, base, count))

    def finish(index, base, count):
        totals = [None, None]
        for c in range(count):
            pl.when(index == 0)(copies[c].wait)
            for parity in range(2):
                left_side, right_side = [], []
                for v in range(c * size // LOW // 2, (c + 1) * size // LOW // 2):
                    for part in range(LOW // LANES):
                        left_side.append(w_ref[parity, v, part])
                    at = (2 * v + parity) * LOW
                    right_side.append(emb_ref[at : at + LOW, :])
                term = jnp.dot(
                    jnp.concatenate(left_side, 1), jnp.concatenate(right_side, 0),
                    preferred_element_type=jnp.float32,
                )
                totals[parity] = term if c == 0 else totals[parity] + term
        for g in range(groups):
            msg = gather_group(base + 2 * g)
            at = 2 * SUB * g
            even, odd = (t[at : at + SUB] + t[at + SUB : at + 2 * SUB] for t in totals)
            pooled = (even + pltpu.roll(odd, per, 0)) / msg[:, width : width + 1]
            first, last = pooled[:, :LANES], pooled[:, LANES:]
            one = jnp.where(upper, first, pltpu.roll(last, per, 0))
            two = jnp.where(upper, pltpu.roll(first, per, 0), last)
            for replica in range(replicas):
                out_ref[(base + 2 * g) * replicas + replica] = one
                out_ref[(base + 2 * g + 1) * replicas + replica] = two

    blocks = sources * per // block
    if blocks == 1:
        one_block(0)
    else:
        pl.loop(0, blocks)(one_block)


def place_kernel(info_ref, by_slot_ref, out_ref):
    queries, members, dim = out_ref.shape
    per = by_slot_ref.shape[1] // 2
    upper = lax.broadcasted_iota(jnp.int32, by_slot_ref.shape[1:], 0) < per
    info = info_ref[0:1, :]
    for member in range(members):
        place = info[0, member]
        one, two = by_slot_ref[2 * place], by_slot_ref[2 * place + 1]
        out_ref[:, member, :LANES] = jnp.where(upper, one, pltpu.roll(two, per, 0))
        out_ref[:, member, LANES:] = jnp.where(upper, pltpu.roll(one, per, 0), two)


def exchange(array):
    shards, replicas = lax.axis_size("tbl"), lax.axis_size("rep")
    group = [int(shard) + shards * replica for shard in block_order(shards) for replica in range(replicas)]
    return lax.all_to_all(
        array, ("rep", "tbl"), split_axis=0, concat_axis=0, axis_index_groups=[group], tiled=True
    )


def per_device(embeddings, raw_ids, id_weights, lengths, table_slot, table_rows):
    places = jnp.asarray(np.argsort(block_order(lax.axis_size("tbl"))), jnp.int32)
    pinned = (embeddings, raw_ids, id_weights, lengths, table_slot, table_rows, places)
    embeddings, raw_ids, id_weights, lengths, table_slot, table_rows, places = (
        pltpu.with_memory_space_constraint(x, pltpu.HBM) for x in pinned
    )
    queries, members, width = raw_ids.shape
    tables = table_slot.shape[0]
    rows, dim = embeddings.shape
    vmem = pl.BlockSpec(memory_space=pltpu.VMEM)
    hbm = pl.BlockSpec(memory_space=pltpu.HBM)
    slots = pltpu.SMEM(table_slot.shape, jnp.int32)
    message, info = pl.pallas_call(
        pack_kernel,
        out_shape=(
            jax.ShapeDtypeStruct((tables, queries, LANES), jnp.float32),
            jax.ShapeDtypeStruct((SUB, LANES), jnp.int32),
        ),
        in_specs=[hbm] * 6,
        out_specs=(vmem, vmem),
        scratch_shapes=[
            slots,
            slots,
            slots,
            pltpu.VMEM(raw_ids.shape, raw_ids.dtype),
            pltpu.VMEM(id_weights.shape, id_weights.dtype),
            pltpu.VMEM(lengths.shape, lengths.dtype),
            pltpu.VMEM((queries * members, LANES), jnp.float32),
            pltpu.SemaphoreType.DMA((6,)),
        ],
        compiler_params=pltpu.CompilerParams(vmem_limit_bytes=4 << 20),
        name="pack",
    )(places, table_slot, table_rows, raw_ids, id_weights, lengths)
    replicas = lax.axis_size("rep")
    split = message.reshape(tables * replicas, queries // replicas, LANES)
    received = exchange(split).reshape(message.shape)
    block = min(BLOCK_BAGS, tables * SUB // 2)
    pooled = pl.pallas_call(
        functools.partial(pool_kernel, width),
        out_shape=jax.ShapeDtypeStruct((tables * replicas, SUB, LANES), jnp.float32),
        in_specs=[vmem, vmem, hbm],
        out_specs=vmem,
        scratch_shapes=[
            pltpu.VMEM(embeddings.shape, embeddings.dtype),
            pltpu.VMEM((2, rows // LOW // 2, LOW // LANES, 2 * block, LANES), jnp.bfloat16),
            pltpu.SemaphoreType.DMA((CHUNKS,)),
        ],
        compiler_params=pltpu.CompilerParams(vmem_limit_bytes=24 << 20),
        name="pool",
    )(info, received, embeddings)
    by_slot = exchange(pooled)
    return pl.pallas_call(
        place_kernel,
        out_shape=jax.ShapeDtypeStruct((queries, members, dim), jnp.float32),
        in_specs=[vmem, vmem],
        out_specs=vmem,
        compiler_params=pltpu.CompilerParams(vmem_limit_bytes=4 << 20),
        name="place",
    )(info, by_slot)


def solution(mesh):
    in_specs = (
        P("tbl", None),
        P("tbl", "rep", None),
        P("tbl", "rep", None),
        P("tbl", "rep"),
        P(),
        P(),
    )
    out_specs = P("tbl", "rep", None)
    return jax.shard_map(
        per_device, mesh=mesh, in_specs=in_specs, out_specs=out_specs, check_vma=False
    )
```

```python
import functools

import jax
import jax.numpy as jnp
import numpy as np
from jax import lax
from jax.experimental import pallas as pl
from jax.experimental.pallas import tpu as pltpu
from jax.sharding import PartitionSpec as P

LANES = 128
HALF = 64
SUB = 8
LOW = 256
BLOCK_BAGS = 64
UNROLL = 4
CHUNKS = 8
PREFIXES = (4, 6, 8)
ORDER_SEED = 1018


def block_order(shards):
    return np.random.RandomState(ORDER_SEED).permutation(shards)


def fetch(pairs, sems):
    copies = [pltpu.make_async_copy(src, dst, sems.at[i]) for i, (src, dst) in enumerate(pairs)]
    for copy in copies:
        copy.start()
    for copy in copies:
        copy.wait()


def pack_kernel(
    place_hbm, slot_hbm, rows_hbm, ids_hbm, weights_hbm, len_hbm, out_ref, info_ref,
    place_ref, slot_ref, rows_ref, ids_ref, weights_ref, len_ref, wide_ref, sems,
):
    pairs = (
        (place_hbm, place_ref), (slot_hbm, slot_ref), (rows_hbm, rows_ref), (ids_hbm, ids_ref),
        (weights_hbm, weights_ref), (len_hbm, len_ref),
    )
    fetch(pairs, sems)
    queries, members, width = ids_ref.shape
    first = lax.axis_index("rep") * members
    wide_ref[:, 0:width] = weights_ref[...].reshape(queries * members, width).astype(jnp.float32)
    flat_ids = ids_ref.reshape(queries * members, width)
    position = lax.broadcasted_iota(jnp.int32, (queries, width), 1)
    counts = len_ref[...]
    out_ref[...] = jnp.zeros_like(out_ref)
    here = lax.axis_index("tbl")
    lane = lax.broadcasted_iota(jnp.int32, (1, LANES), 1)

    def find(k, table):
        return jnp.where(slot_ref[k] == here, k, table)

    table = lax.fori_loop(0, slot_ref.shape[0], find, jnp.int32(0), unroll=slot_ref.shape[0] <= 16)
    info_ref[1:2, :] = jnp.full((1, LANES), table // members, jnp.int32)
    info_ref[2:3, :] = jnp.full((1, LANES), rows_ref[table], jnp.int32)
    mine = jnp.zeros((1, LANES), jnp.int32)
    for member in range(members):
        place = place_ref[slot_ref[first + member]]
        mine = jnp.where(lane == member, place, mine)
        rows = jnp.full((queries, width), rows_ref[first + member], jnp.int32).astype(jnp.float32)
        ids = flat_ids[pl.ds(member, queries, stride=members), :].astype(jnp.float32)
        local = ids - jnp.floor((ids + 0.5) * (1.0 / rows)) * rows
        count = counts[:, member : member + 1]
        weights = wide_ref[pl.ds(member, queries, stride=members), 0:width]
        weights = jnp.where(position < count, weights, 0.0)
        out_ref[place, :, 0:width] = local
        out_ref[place, :, width : width + 1] = count.astype(jnp.float32)
        out_ref[place, :, HALF : HALF + width] = weights
    info_ref[0:1, :] = mine


def pool_kernel(width, info_ref, msg_ref, emb_hbm, out_ref, emb_ref, w_ref, sems):
    rows, dim = emb_ref.shape
    highs = rows // LOW
    chunks = sems.shape[0]
    size = rows // chunks
    copies = [
        pltpu.make_async_copy(emb_hbm.at[pl.ds(c * size, size)], emb_ref.at[pl.ds(c * size, size)], sems.at[c])
        for c in range(chunks)
    ]
    for copy in copies[: PREFIXES[0]]:
        copy.start()
    used = info_ref[2:3, :][0, 0]

    def within(part):
        low_end = 0 if part == 0 else PREFIXES[part - 1] * size
        above = used > low_end
        return above if part == len(PREFIXES) - 1 else above & (used <= PREFIXES[part] * size)

    for part in range(1, len(PREFIXES)):

        @pl.when(used > PREFIXES[part - 1] * size)
        def _(part=part):
            for copy in copies[PREFIXES[part - 1] : PREFIXES[part]]:
                copy.start()

    sources = msg_ref.shape[0]
    replicas = lax.axis_size("rep")
    per = SUB // replicas
    block = min(BLOCK_BAGS, sources * per)
    groups = block // SUB
    lane = lax.broadcasted_iota(jnp.int32, (SUB, LANES), 1)
    sub = lax.broadcasted_iota(jnp.int32, (SUB, LANES), 0)
    left = lane < HALF
    upper = sub < per
    first_owner = jnp.broadcast_to(info_ref[1:2, :], (SUB, LANES)) == 0
    owns = [sub % per == jnp.where(left, 2 * m, 2 * m + 1) for m in range(2)]
    low_iota = lax.broadcasted_iota(jnp.int32, (LOW, LANES), 0).astype(jnp.float32).astype(jnp.bfloat16)

    def gather_group(start):
        one, two = msg_ref[start], msg_ref[start + 1]
        low_half = jnp.where(upper, one, pltpu.roll(two, per, 0))
        high_half = jnp.where(upper, pltpu.roll(one, per, 0), two)
        return jnp.where(first_owner, low_half, high_half)

    def spread_four(high, low, weights, flip, base):
        lhs, rhs = [], []
        shift = jnp.where(upper, 1.0, 0.0) if flip else jnp.where(upper, 0.0, 1.0)
        for m in range(2):
            h = jnp.where(owns[m], high - shift, -100.0)
            h = jnp.concatenate([h, h - 2.0], 0).astype(jnp.bfloat16)
            w = jnp.where(owns[m], weights, 0.0)
            w = jnp.concatenate([w, w], 0).astype(jnp.bfloat16)
            lhs.append(
                jnp.concatenate(
                    [jnp.where(h == jnp.bfloat16(top), w, jnp.bfloat16(0)) for top in range(0, highs, 4)], 0
                )
            )
            at = base + 2 * m
            row = jnp.where(left[0:1], low[at : at + 1], low[at + 1 : at + 2])
            row = jnp.broadcast_to(row, (2 * SUB, LANES)).astype(jnp.bfloat16)
            row = jnp.concatenate([row] * (LOW // (2 * SUB)), 0)
            rhs.append(jnp.where(low_iota == row, jnp.bfloat16(1), jnp.bfloat16(0)))
        return lax.dot_general(
            jnp.concatenate(lhs, 1), jnp.concatenate(rhs, 1), (((1,), (1,)), ((), ())),
            preferred_element_type=jnp.float32,
        )

    def one_block(index):
        base = index * (block // per)

        def one_group(g):
            msg = gather_group(base + 2 * g)
            turned = pltpu.roll(msg, HALF, 1)
            ids = jnp.where(left, msg, turned)
            weights = jnp.where(left, turned, msg)
            high = jnp.floor(ids * (1.0 / LOW))
            low = ids - high * LOW
            high_turned = pltpu.roll(high, per, 0)
            weights_turned = pltpu.roll(weights, per, 0)
            one = spread_four(
                jnp.where(upper, high, high_turned), low, jnp.where(upper, weights, weights_turned), False, 0
            )
            two = spread_four(
                jnp.where(upper, high_turned, high), low, jnp.where(upper, weights_turned, weights), True, per
            )
            at = pl.ds(pl.multiple_of(g * 2 * SUB, 2 * SUB), 2 * SUB)
            for v in range(highs // 2):
                for part in range(LOW // LANES):
                    cut = (slice(v * SUB, (v + 1) * SUB), slice(part * LANES, (part + 1) * LANES))
                    even = jnp.where(upper, one[cut], two[cut])
                    odd = jnp.where(upper, two[cut], one[cut])
                    both = jnp.concatenate([even, odd], 0)
                    rest = both - both.astype(jnp.bfloat16).astype(jnp.float32)
                    w_ref[0, v, part, at, :] = jnp.concatenate([even, rest[:SUB]], 0).astype(jnp.bfloat16)
                    w_ref[1, v, part, at, :] = jnp.concatenate([odd, rest[SUB:]], 0).astype(jnp.bfloat16)

        def body(g, carry):
            for u in range(UNROLL):
                one_group(g * UNROLL + u)
            return carry

        if groups == UNROLL:
            body(0, 0)
        else:
            lax.fori_loop(0, groups // UNROLL, body, 0)
        for part, count in enumerate(PREFIXES):
            pl.when(within(part))(functools.partial(finish, index, base, count))

    def finish(index, base, count):
        totals = [None, None]
        for c in range(count):
            pl.when(index == 0)(copies[c].wait)
            for parity in range(2):
                left_side, right_side = [], []
                for v in range(c * size // LOW // 2, (c + 1) * size // LOW // 2):
                    for part in range(LOW // LANES):
                        left_side.append(w_ref[parity, v, part])
                    at = (2 * v + parity) * LOW
                    right_side.append(emb_ref[at : at + LOW, :])
                term = jnp.dot(
                    jnp.concatenate(left_side, 1), jnp.concatenate(right_side, 0),
                    preferred_element_type=jnp.float32,
                )
                totals[parity] = term if c == 0 else totals[parity] + term
        for g in range(groups):
            msg = gather_group(base + 2 * g)
            at = 2 * SUB * g
            even, odd = (t[at : at + SUB] + t[at + SUB : at + 2 * SUB] for t in totals)
            pooled = (even + pltpu.roll(odd, per, 0)) / msg[:, width : width + 1]
            first, last = pooled[:, :LANES], pooled[:, LANES:]
            one = jnp.where(upper, first, pltpu.roll(last, per, 0))
            two = jnp.where(upper, pltpu.roll(first, per, 0), last)
            for replica in range(replicas):
                out_ref[(base + 2 * g) * replicas + replica] = one
                out_ref[(base + 2 * g + 1) * replicas + replica] = two

    blocks = sources * per // block
    if blocks == 1:
        one_block(0)
    else:
        pl.loop(0, blocks)(one_block)


def place_kernel(info_ref, by_slot_ref, out_ref):
    queries, members, dim = out_ref.shape
    per = by_slot_ref.shape[1] // 2
    upper = lax.broadcasted_iota(jnp.int32, by_slot_ref.shape[1:], 0) < per
    info = info_ref[0:1, :]
    for member in range(members):
        place = info[0, member]
        one, two = by_slot_ref[2 * place], by_slot_ref[2 * place + 1]
        out_ref[:, member, :LANES] = jnp.where(upper, one, pltpu.roll(two, per, 0))
        out_ref[:, member, LANES:] = jnp.where(upper, pltpu.roll(one, per, 0), two)


def exchange(array):
    shards, replicas = lax.axis_size("tbl"), lax.axis_size("rep")
    group = [int(shard) + shards * replica for shard in block_order(shards) for replica in range(replicas)]
    return lax.all_to_all(
        array, ("rep", "tbl"), split_axis=0, concat_axis=0, axis_index_groups=[group], tiled=True
    )


def per_device(embeddings, raw_ids, id_weights, lengths, table_slot, table_rows):
    places = jnp.asarray(np.argsort(block_order(lax.axis_size("tbl"))), jnp.int32)
    pinned = (embeddings, raw_ids, id_weights, lengths, table_slot, table_rows, places)
    embeddings, raw_ids, id_weights, lengths, table_slot, table_rows, places = (
        pltpu.with_memory_space_constraint(x, pltpu.HBM) for x in pinned
    )
    queries, members, width = raw_ids.shape
    tables = table_slot.shape[0]
    rows, dim = embeddings.shape
    vmem = pl.BlockSpec(memory_space=pltpu.VMEM)
    hbm = pl.BlockSpec(memory_space=pltpu.HBM)
    slots = pltpu.SMEM(table_slot.shape, jnp.int32)
    message, info = pl.pallas_call(
        pack_kernel,
        out_shape=(
            jax.ShapeDtypeStruct((tables, queries, LANES), jnp.float32),
            jax.ShapeDtypeStruct((SUB, LANES), jnp.int32),
        ),
        in_specs=[hbm] * 6,
        out_specs=(vmem, vmem),
        scratch_shapes=[
            slots,
            slots,
            slots,
            pltpu.VMEM(raw_ids.shape, raw_ids.dtype),
            pltpu.VMEM(id_weights.shape, id_weights.dtype),
            pltpu.VMEM(lengths.shape, lengths.dtype),
            pltpu.VMEM((queries * members, LANES), jnp.float32),
            pltpu.SemaphoreType.DMA((6,)),
        ],
        compiler_params=pltpu.CompilerParams(vmem_limit_bytes=4 << 20),
        name="pack",
    )(places, table_slot, table_rows, raw_ids, id_weights, lengths)
    replicas = lax.axis_size("rep")
    split = message.reshape(tables * replicas, queries // replicas, LANES)
    received = exchange(split).reshape(message.shape)
    block = min(BLOCK_BAGS, tables * SUB // 2)
    pooled = pl.pallas_call(
        functools.partial(pool_kernel, width),
        out_shape=jax.ShapeDtypeStruct((tables * replicas, SUB, LANES), jnp.float32),
        in_specs=[vmem, vmem, hbm],
        out_specs=vmem,
        scratch_shapes=[
            pltpu.VMEM(embeddings.shape, embeddings.dtype),
            pltpu.VMEM((2, rows // LOW // 2, LOW // LANES, 2 * block, LANES), jnp.bfloat16),
            pltpu.SemaphoreType.DMA((CHUNKS,)),
        ],
        compiler_params=pltpu.CompilerParams(vmem_limit_bytes=24 << 20),
        name="pool",
    )(info, received, embeddings)
    by_slot = exchange(pooled)
    return pl.pallas_call(
        place_kernel,
        out_shape=jax.ShapeDtypeStruct((queries, members, dim), jnp.float32),
        in_specs=[vmem, vmem],
        out_specs=vmem,
        compiler_params=pltpu.CompilerParams(vmem_limit_bytes=4 << 20),
        name="place",
    )(info, by_slot)


def solution(mesh):
    in_specs = (
        P("tbl", None),
        P("tbl", "rep", None),
        P("tbl", "rep", None),
        P("tbl", "rep"),
        P(),
        P(),
    )
    out_specs = P("tbl", "rep", None)
    return jax.shard_map(
        per_device, mesh=mesh, in_specs=in_specs, out_specs=out_specs, check_vma=False
    )
```
